32 devices in a mesh: rep: 8 (over y, x, core), fsdp: 4 (over z).
Axes of the slice: x: 2, y: 2, z: 4, core: 2. Of those that a mesh axis runs over, the one named last changes fastest.
Arguments:
- images: bfloat16 [8, 16, 128, 768], P('rep', 'fsdp'), may hold values from -6 to 6
- cotangent: bfloat16 [8, 16, 128, 1536], P('rep', 'fsdp'), may hold values from -6 to 6
- params: float32 [8, 768, 1536], P('rep', 'fsdp'), may hold values from -6 to 6
- counts: int32 [8, 4], P('rep'), may hold values from 1 to 4, 9 in all within a row
- partner: int32 [8], P('rep'), may hold values from 0 to 7, as said below
- ln_gain: float32 [768], replicated, may hold values from 0.1 to 1.9
- ln_bias: float32 [768], replicated, may hold values from -3 to 3
- expand_bias: float32 [1536], replicated, may hold values from -4 to 4
Outputs:
- new_params: float32 [8, 768, 1536], P('rep', 'fsdp')
The draws below stay inside these ranges and needn't reach their ends.
Inputs may be any that keep to these rules, and one draw needn't show every extreme that they name: The 4 counts of a replica sum to 9; some group holds 4 live images. partner[partner[r]] equals r, and partner[r] is r or (r + 4) modulo 8.
All inputs are finite; a program needn't handle non-finite values.
Results may differ from the reference program's by a relative error of at most 0.0045.
Values may be sent and summed in bfloat16 or wider, within the bound.
A program may use at most 64 MiB of HBM per device.

```python
import math
import jax
import jax.numpy as jnp
import numpy as np
from jax import lax

C = 768
HID = 1536
IMG_DEV = 4
ROWS_IMG = 128
REPS = 8
LIVE = 9
N_FSDP = 4


def draw_partner(key, part):
    half_count = REPS // 2
    active = jax.random.randint(jax.random.fold_in(key, 12), (half_count,), 0, 4) > 0
    position = jnp.arange(REPS, dtype=jnp.int32)
    pair_slot = position % half_count
    opposite = (position + half_count) % REPS
    return jnp.where(active[pair_slot], opposite, position).astype(jnp.int32)


def block_scale(own_key, shape, cuts, low, top_value):
    factor_of, own = 1.0, jax.random.fold_in(own_key, 6)
    for dim, shards_of in cuts:
        draws = jnp.exp(jax.random.uniform(jax.random.fold_in(own, dim), (shards_of,), jnp.float32, low / len(cuts), top_value / len(cuts)))
        factor_of = factor_of * jnp.repeat(draws, shape[dim] // shards_of).reshape([-1 if axis == dim else 1 for axis in range(len(shape))])
    return factor_of


def profile(number_of, total, reach, skew):
    loads = [(1 << 20) // math.isqrt(standing ** skew) + 1 for standing in range(2, number_of + 1)]
    spare, holding = total - reach - (number_of - 1), [1] * (number_of - 1)
    while spare > 0:
        candidates = [i for i in range(number_of - 1) if holding[i] < reach]
        whole, budget = sum([loads[i] for i in candidates]), spare
        for i in candidates:
            more = min(reach - holding[i], max(1, budget * loads[i] // whole), spare)
            holding[i] = holding[i] + more
            spare = spare - more
    return np.array([reach] + holding)


def ragged_sizes(rng, number_of, total, most, lean):
    if number_of == 2:
        one = jax.random.randint(rng, (), max(1, total - most), min(most, total - 1) + 1)
        return jnp.stack([one, total - one])
    sizes = jnp.asarray(profile(number_of, total, most, lean), jnp.int32)
    twos = (number_of - 1) // 2
    donor, sink = sizes[1:1 + 2 * twos:2], sizes[2:2 + 2 * twos:2]
    slack = jnp.minimum(donor - 1, most - sink)
    shifted = jax.random.randint(jax.random.fold_in(rng, 1), (twos,), 0, 1 << 20) % (slack + 1)
    sizes = sizes.at[1:1 + 2 * twos:2].set(donor - shifted).at[2:2 + 2 * twos:2].set(sink + shifted)
    return sizes[jax.random.permutation(jax.random.fold_in(rng, 2), number_of)]


def normal_values(key, shape, width, most, split=(), kind=jnp.bfloat16):
    array = width * jax.random.normal(key, shape, jnp.float32)
    if split:
        array = array * block_scale(key, shape, split, -0.22, 0.18)
    return jnp.clip(array, -most, most).astype(kind)


def setup_inputs(seed: int = 0) -> dict:
    key_list = jax.random.split(jax.random.key(seed), 9)
    images = normal_values(key_list[0], (REPS, N_FSDP * IMG_DEV, ROWS_IMG, C), 1.0, 6.0, ((0, 8), (1, 4)))
    cotangent = normal_values(key_list[1], (REPS, N_FSDP * IMG_DEV, ROWS_IMG, HID), 1.0, 6.0, ((0, 8), (1, 4)))
    params = normal_values(key_list[2], (REPS, C, HID), 1.0, 6.0, ((0, 8), (1, 4)), jnp.float32)
    counts = jax.vmap(lambda own: ragged_sizes(own, N_FSDP, LIVE, IMG_DEV, 2))(jax.random.split(key_list[3], REPS)).reshape((REPS, N_FSDP)).astype(jnp.int32)
    partner = draw_partner(jax.random.fold_in(key_list[8], 71), 0)
    ln_gain = jnp.clip(1.0 + 0.18 * jax.random.normal(key_list[5], (C,), jnp.float32), 0.1, 1.9)
    ln_bias = normal_values(key_list[6], (C,), 0.5, 3.0, (), jnp.float32)
    expand_bias = normal_values(key_list[7], (HID,), 1.0, 4.0, (), jnp.float32)
    return dict(images=images, cotangent=cotangent, params=params, counts=counts, partner=partner, ln_gain=ln_gain, ln_bias=ln_bias, expand_bias=expand_bias)


eps_norm = 1e-06
learn_rate = 0.5

def normalize(rows, ln_gain, ln_bias):
    row_mean = lax.optimization_barrier(jnp.mean(rows, axis=-1, keepdims=True))
    centered = rows - row_mean
    variance = lax.optimization_barrier(jnp.mean(centered * centered, axis=-1, keepdims=True))
    return centered * lax.rsqrt(variance + eps_norm) * ln_gain + ln_bias

def exact_gelu(values):
    return jax.nn.gelu(values, approximate=False)

def gelu_slope(pre, upstream):
    outputs, pull = jax.vjp(exact_gelu, pre)
    return pull(upstream)[0]

def reference(images, cotangent, params, counts, partner, ln_gain, ln_bias, expand_bias):
    scale = float(C) ** (-0.5)
    group_rows = IMG_DEV * ROWS_IMG

    def one_replica(items):
        image_block, cot_block, weights, count_row = items
        low_weights = weights.astype(jnp.bfloat16)
        normed_all = normalize(image_block.astype(jnp.float32).reshape(N_FSDP, group_rows, C), ln_gain, ln_bias).astype(jnp.bfloat16)
        cot_all = cot_block.reshape(N_FSDP, group_rows, HID).astype(jnp.float32)
        slot_of_row = jnp.arange(group_rows, dtype=jnp.int32) // ROWS_IMG
        gradient = jnp.zeros((C, HID), jnp.float32)
        for member in range(N_FSDP):
            pre = jnp.dot(normed_all[member], low_weights, preferred_element_type=jnp.float32) * scale + expand_bias
            live = (slot_of_row < count_row[member]).astype(jnp.float32)
            delta = (gelu_slope(pre, cot_all[member]) * live[:, None]).astype(jnp.bfloat16)
            partial_term = lax.dot_general(normed_all[member], delta, (((0,), (0,)), ((), ())), preferred_element_type=jnp.float32) * scale
            rounded = lax.optimization_barrier(partial_term.astype(jnp.bfloat16))
            gradient = gradient + rounded.astype(jnp.float32)
        return weights - learn_rate * gradient
    stepped = lax.map(one_replica, (images, cotangent, params, counts))
    return (stepped + jnp.take(stepped, partner.astype(jnp.int32), axis=0)) * 0.5
```

```python
import functools

import jax
import jax.numpy as jnp
from jax import lax
from jax.experimental import pallas as pl
from jax.experimental.pallas import tpu as pltpu
from jax.sharding import PartitionSpec as P

eps_norm = 1e-06
learn_rate = 0.5
CHUNK = 128
DEPTH = 1.0
PRI = dict(
    own=-13.95, fwd=-13.04, fwd_far=-4.93, comp=-1.0, sum=-2.09, sum_far=-6.79, sum_hop=13.66,
    fin=-5.34, merge=-2.93, norm=10.81,
)
MESH_ID = pl.DeviceIdType.MESH


def plan(n, widths, pri, depth, rate=120.0, lat=2.2, cost=0.06):
    last = n - 1
    pieces = len(widths)
    dur = [w / rate + cost for w in widths]
    arrive = [dict() for _ in range(n)]
    now = [2.0] * n
    link = [dict(u=0.0, d=0.0, y=0.0) for _ in range(n)]
    todo, orders = [], [[] for _ in range(n)]
    for z in range(n):
        mine = []
        for k in range(pieces):
            if z < last: mine.append(("own", k, z, "u"))
            if z > 0: mine.append(("own", k, z, "d"))
            for s in range(n):
                if s != z: mine.append(("fwd", k, s, "u" if s < z else "d"))
            mine.append(("comp", k, 0, ""))
            for j in range(z + 1, n): mine.append(("sum", k, j, "u"))
            for j in range(z): mine.append(("sum", k, j, "d"))
            mine.append(("fin", k, z, "y"))
            mine.append(("merge", k, z, ""))
        mine.append(("norm", 0, 0, ""))
        todo.append(mine)
    done = [set() for _ in range(n)]
    def rank(z, t):
        kind, k, j, way = t
        far = abs(j - z)
        if kind == "own": return k + pri["own"]
        if kind == "fwd": return k + pri["fwd"] + (far - 1) * pri["fwd_far"]
        if kind == "sum": return k + pri["sum"] + far * pri["sum_far"] + (z if way == "u" else last - z) * pri["sum_hop"]
        return k + pri.get(kind, 0.0)
    def ready(z, t):
        kind, k, j, way = t
        a, d = arrive[z], done[z]
        times = [0.0]
        inf = float("inf")
        if kind == "fwd":
            times.append(a.get(("a", k, j), inf))
        elif kind == "comp":
            if ("norm", 0, 0, "") not in d: return inf
            if k and ("comp", k - 1, 0, "") not in d: return inf
            for s in range(n):
                if s != z and ("fwd", k, s, "u" if s < z else "d") not in d: return inf
        elif kind in ("sum", "fin"):
            if ("comp", k, 0, "") not in d: return inf
            if kind == "sum" and (z > 0 if way == "u" else z < last): times.append(a.get((way, k, j), inf))
            if kind == "fin":
                if z > 0: times.append(a.get(("u", k, z), inf))
                if z < last: times.append(a.get(("d", k, z), inf))
        elif kind == "merge":
            if ("fin", k, z, "y") not in d: return inf
            times.append(a.get(("y", k, z), inf))
        sends = kind in ("own", "sum") or (kind == "fwd" and (z < last if way == "u" else z > 0))
        if sends: times.append(link[z][way] - depth * dur[k])
        return max(times)
    while any(todo):
        best = None
        for z in range(n):
            if not todo[z]: continue
            r = [(ready(z, t), t) for t in todo[z]]
            t0 = max(now[z], min(r)[0])
            if t0 == float("inf"): continue
            if best is None or t0 < best[0]:
                best = (t0, z, min((t for e, t in r if e <= t0), key=lambda t: (rank(z, t), t)))
        t0, z, t = best
        kind, k, j, way = t
        todo[z].remove(t); done[z].add(t); orders[z].append(t)
        spend = {"own": .03, "fwd": .05, "comp": widths[k] / 110.0, "sum": .12, "fin": .15, "merge": .15, "norm": 2.0}[kind]
        now[z] = t0 + spend
        to = None
        if kind == "own" or kind == "fwd": to, tag = z + (1 if way == "u" else -1), ("a", k, j)
        elif kind == "sum": to, tag = z + (1 if way == "u" else -1), (way, k, j)
        elif kind == "fin": to, tag = z, ("y", k, z)
        if to is not None and 0 <= to <= last:
            start = max(link[z][way], now[z])
            link[z][way] = start + dur[k]
            arrive[to][tag] = start + dur[k] + lat
    return max(now), orders


def gelu_slope(x):
    cdf = 0.5 * (1.0 + lax.erf(x * 0.7071067811865476))
    return cdf + x * (jnp.exp(-0.5 * x * x) * 0.3989422804014327)


def body(
    n, reps, pieces,
    partner_ref, count_in, images, cotangent, weights, gain_in, bias_in, ebias_in,
    out_ref,
    gain_ref, bias_ref, ebias_ref, img, cot, par, x, xt, wfull, delta, part, u_in, d_in, u_out, d_out, acc,
    far_out, far_in,
    count_ref, in_sem, z_recv, y_recv, sent,
):
    z = lax.axis_index("fsdp")
    rep = lax.axis_index("rep")
    partner = {"rep": lax.rem(rep + reps // 2, reps)}
    up, down = {"fsdp": z + 1}, {"fsdp": z - 1}
    last = n - 1
    slots, per_image, width = images.shape
    depth = width // n
    cols = wfull.shape[-1]
    scale = float(width) ** (-0.5)

    _, orders = plan(n, [cols] * pieces, PRI, DEPTH)
    segments = []
    for order in orders:
        parts = [[]]
        for entry in order:
            if entry[0] in ("norm", "comp"):
                parts.append([])
            else:
                parts[-1].append(entry)
        segments.append(parts)
    early = 1 + max(entry[1] for parts in segments for entry in parts[0])

    def load_cols(lo, hi, sem):
        span = pl.ds(lo * cols, (hi - lo) * cols)
        return pltpu.make_async_copy(weights.at[:, span], par.at[:, span], sem)

    load_w = load_cols(0, early, in_sem.at[0])
    load_rest = load_cols(early, pieces, in_sem.at[6])
    load_x = pltpu.make_async_copy(images, img, in_sem.at[1])
    load_c = pltpu.make_async_copy(cotangent, cot, in_sem.at[2])
    small = [
        pltpu.make_async_copy(gain_in, gain_ref, in_sem.at[3]),
        pltpu.make_async_copy(bias_in, bias_ref, in_sem.at[4]),
        pltpu.make_async_copy(ebias_in, ebias_ref, in_sem.at[5]),
        pltpu.make_async_copy(count_in, count_ref, in_sem.at[7]),
    ]
    load_w.start()

    barrier = pltpu.get_barrier_semaphore()

    @pl.when(z < last)
    def _():
        pl.semaphore_signal(barrier, inc=1, device_id=up, device_id_type=MESH_ID)

    @pl.when(z > 0)
    def _():
        pl.semaphore_signal(barrier, inc=1, device_id=down, device_id_type=MESH_ID)

    pl.semaphore_signal(barrier, inc=1, device_id=partner, device_id_type=MESH_ID)

    load_rest.start()
    load_x.start()
    for load in small:
        load.start()
    load_c.start()

    def cast(k):
        wfull[k, z] = par[:, k * cols:(k + 1) * cols].astype(jnp.bfloat16)

    load_w.wait()
    for k in range(early):
        cast(k)

    peers = 1 + (z > 0).astype(jnp.int32) + (z < last).astype(jnp.int32)
    pl.semaphore_wait(barrier, peers)

    def remote(src, dst, send, recv, to):
        return pltpu.make_async_remote_copy(
            src_ref=src, dst_ref=dst, send_sem=send, recv_sem=recv,
            device_id=to, device_id_type=MESH_ID,
        )

    ag_up, ag_dn, u_send, d_send, y_send = (sent.at[i] for i in range(5))

    def ag_copy(k, s, to, send):
        return remote(wfull.at[k, s], wfull.at[k, s], send, z_recv.at[k, s], to)

    def u_copy(k, j, here):
        return remote(u_out.at[k, j], u_in.at[k, j], u_send, z_recv.at[k, j], up)

    def d_copy(k, j, here):
        sem = z_recv.at[k, n if j == here else j]
        return remote(d_out.at[k, j], d_in.at[k, j], d_send, sem, down)

    def y_copy(k):
        return remote(far_out.at[k], far_in.at[k], y_send, y_recv.at[k], partner)

    def norm():
        load_rest.wait()
        for k in range(early, pieces):
            cast(k)
        load_x.wait()
        for load in small:
            load.wait()
        gain = gain_ref[...][None, :]
        shift = bias_ref[...][None, :]
        for i in range(slots):
            rows = img[i].astype(jnp.float32)
            mean = jnp.mean(rows, axis=-1, keepdims=True)
            centered = rows - mean
            var = jnp.mean(centered * centered, axis=-1, keepdims=True)
            v = centered * lax.rsqrt(var + eps_norm) * gain + shift
            x[i] = v.astype(jnp.bfloat16)
            xt[:, i * per_image:(i + 1) * per_image] = v.T.astype(jnp.bfloat16)
        load_c.wait()

    def mix():
        return jnp.where(partner_ref[0] != rep, 0.5, 0.0).astype(jnp.float32)

    def compute(k):
        lo = k * cols
        w = wfull.at[k]
        extra = ebias_ref[lo:lo + cols][None, :]

        def one(i, carry):
            pre = jnp.dot(
                x[i], w[...].reshape(width, cols), preferred_element_type=jnp.float32
            )
            pre = pre * scale + extra
            live = jnp.where(i < count_ref[0, z], 1.0, 0.0).astype(jnp.float32)
            cur = cot[i, :, lo:lo + cols].astype(jnp.float32)
            rows = pl.ds(pl.multiple_of(i * per_image, per_image), per_image)
            delta[rows, :] = (cur * gelu_slope(pre) * live).astype(jnp.bfloat16)
            return carry

        lax.fori_loop(0, slots, one, 0)

        def two(j, carry):
            rows = pl.ds(pl.multiple_of(j * depth, depth), depth)
            part[k, j] = scale * jnp.dot(
                xt[rows, :], delta[...], preferred_element_type=jnp.float32
            )
            return carry

        lax.fori_loop(0, n, two, 0)

    def step(me, kind, k, j, way):
        to, send = (up, ag_up) if way == "u" else (down, ag_dn)
        copy, came, out = (u_copy, u_in, u_out) if way == "u" else (d_copy, d_in, d_out)
        final = me == (last if way == "u" else 0)
        first = me == (0 if way == "u" else last)
        if kind == "own":
            ag_copy(k, me, to, send).start()
        elif kind == "fwd":
            ag_copy(k, j, to, send).wait_recv()
            if not final:
                ag_copy(k, j, to, send).start()
        elif kind == "sum":
            total = part[k, j]
            if not first:
                copy(k, j, me).wait_recv()
                total = total + came[k, j].astype(jnp.float32)
            out[k, j] = total.astype(jnp.bfloat16)
            copy(k, j, me + 1 if way == "u" else me - 1).start()
        elif kind == "fin":
            total = part[k, me]
            if me > 0:
                u_copy(k, me, me).wait_recv()
                total = total + u_in[k, me].astype(jnp.float32)
            if me < last:
                d_copy(k, me, me).wait_recv()
                total = total + d_in[k, me].astype(jnp.float32)
            stepped = par[:, k * cols:(k + 1) * cols] - learn_rate * total
            acc[k] = stepped
            far_out[k] = stepped.astype(jnp.bfloat16)
            y_copy(k).start()
        elif kind == "merge":
            y_copy(k).wait_recv()
            stepped = acc[k]
            out_ref[:, k * cols:(k + 1) * cols] = stepped + mix() * (far_in[k].astype(jnp.float32) - stepped)

    for stage in range(pieces + 2):
        for me in range(n):
            @pl.when(z == me)
            def _():
                for entry in segments[me][stage]:
                    step(me, *entry)
        if stage == 0:
            norm()
        elif stage <= pieces:
            compute(stage - 1)

    def drain(ref, send):
        remote(ref, ref, send, y_recv.at[0], partner).wait_send()

    for me in range(n):
        @pl.when(z == me)
        def _():
            if me < last:
                drain(wfull.at[:, :me + 1], ag_up)
                drain(u_out.at[:, me + 1:], u_send)
            if me > 0:
                drain(wfull.at[:, me:], ag_dn)
                drain(d_out.at[:, :me], d_send)
    drain(far_out, y_send)


def shards(n, reps, images, cotangent, params, counts, partner, ln_gain, ln_bias, expand_bias):
    _, slots, per_image, width = images.shape
    hidden = cotangent.shape[-1]
    depth = params.shape[1]
    cols = CHUNK
    pieces = hidden // cols
    rows = slots * per_image
    anywhere = pl.BlockSpec(memory_space=pl.ANY)
    dma = pltpu.SemaphoreType.DMA
    bf, f32 = jnp.bfloat16, jnp.float32
    piece = (pieces, n, depth, cols)
    merged = pl.pallas_call(
        functools.partial(body, n, reps, pieces),
        out_shape=pltpu.VMEM((depth, hidden), f32),
        in_specs=[pl.BlockSpec(memory_space=pltpu.SMEM)] + [anywhere] * 7,
        out_specs=pl.BlockSpec(memory_space=pltpu.VMEM),
        scratch_shapes=[
            pltpu.VMEM((width,), f32),
            pltpu.VMEM((width,), f32),
            pltpu.VMEM((hidden,), f32),
            pltpu.VMEM((slots, per_image, width), bf),
            pltpu.VMEM((slots, per_image, hidden), bf),
            pltpu.VMEM((depth, hidden), f32),
            pltpu.VMEM((slots, per_image, width), bf),
            pltpu.VMEM((width, rows), bf),
            pltpu.VMEM(piece, bf),
            pltpu.VMEM((rows, cols), bf),
            pltpu.VMEM(piece, f32),
            pltpu.VMEM(piece, bf),
            pltpu.VMEM(piece, bf),
            pltpu.VMEM(piece, bf),
            pltpu.VMEM(piece, bf),
            pltpu.VMEM((pieces, depth, cols), f32),
            pltpu.VMEM((pieces, depth, cols), bf),
            pltpu.VMEM((pieces, depth, cols), bf),
            pltpu.SMEM((1, n), jnp.int32),
            dma((8,)), dma((pieces, n + 1)), dma((pieces,)), dma((5,)),
        ],
        compiler_params=pltpu.CompilerParams(
            collective_id=0, has_side_effects=True, vmem_limit_bytes=32 * 1024 * 1024
        ),
    )(
        partner, *[
            pltpu.with_memory_space_constraint(array, pltpu.HBM)
            for array in (
                counts, images[0], cotangent[0], params[0], ln_gain, ln_bias, expand_bias,
            )
        ],
    )
    return merged[None]


def solution(mesh):
    in_specs = (
        P("rep", "fsdp", None, None),
        P("rep", "fsdp", None, None),
        P("rep", "fsdp", None),
        P("rep", None),
        P("rep"),
        P(),
        P(),
        P(),
    )
    out_specs = P("rep", "fsdp", None)
    return jax.shard_map(
        functools.partial(shards, mesh.shape["fsdp"], mesh.shape["rep"]),
        mesh=mesh, in_specs=in_specs, out_specs=out_specs, check_vma=False,
    )
```

```python
import functools

import jax
import jax.numpy as jnp
from jax import lax
from jax.experimental import pallas as pl
from jax.experimental.pallas import tpu as pltpu
from jax.sharding import PartitionSpec as P

eps_norm = 1e-06
learn_rate = 0.5
CHUNK = 128
DEPTH = 1.0
MIXED = (1, 5, 8)
PRI = dict(
    give=192.27, take=-47.75, late=95.14, own=-10.17, fwd=-5.93, fwd_far=-0.75, comp=50.94, sum=78.09, sum_far=-82.25, sum_hop=50.75, fin=-114.91, merge=-80.50, norm=68.37,
)
MESH_ID = pl.DeviceIdType.MESH


def plan(n, widths, pri, depth, mixed, rate=125.0, lat=2.5, cost=0.055):
    last = n - 1
    pieces = len(widths)
    dur = [w / rate + cost for w in widths]
    arrive = [dict() for _ in range(n)]
    now = [2.0] * n
    link = [dict(u=0.0, d=0.0, y=0.0) for _ in range(n)]
    todo, orders = [], [[] for _ in range(n)]
    for z in range(n):
        mine = []
        for k in range(pieces):
            if z < last: mine.append(("own", k, z, "u"))
            if z > 0: mine.append(("own", k, z, "d"))
            for s in range(n):
                if s != z: mine.append(("fwd", k, s, "u" if s < z else "d"))
            mine.append(("comp", k, 0, ""))
            for j in range(z + 1, n): mine.append(("sum", k, j, "u"))
            for j in range(z): mine.append(("sum", k, j, "d"))
            mine.append(("fin", k, z, "y"))
            if k in mixed:
                mine.append(("give", k, z, "y"))
                mine.append(("take", k, z, ""))
            else:
                mine.append(("merge", k, z, ""))
        mine.append(("norm", 0, 0, ""))
        todo.append(mine)
    done = [set() for _ in range(n)]
    def rank(z, t):
        kind, k, j, way = t
        far = abs(j - z)
        if kind == "own": return k + pri["own"]
        if kind == "fwd": return k + pri["fwd"] + (far - 1) * pri["fwd_far"]
        if kind == "sum": return k + (pri["late"] if k in mixed else 0.0) + pri["sum"] + far * pri["sum_far"] + (z if way == "u" else last - z) * pri["sum_hop"]
        return k + pri.get(kind, 0.0)
    def ready(z, t):
        kind, k, j, way = t
        a, d = arrive[z], done[z]
        times = [0.0]
        inf = float("inf")
        if kind == "fwd":
            times.append(a.get(("a", k, j), inf))
        elif kind == "comp":
            if ("norm", 0, 0, "") not in d: return inf
            if k and ("comp", k - 1, 0, "") not in d: return inf
            for s in range(n):
                if s != z and ("fwd", k, s, "u" if s < z else "d") not in d: return inf
        elif kind in ("sum", "fin", "give"):
            if ("comp", k, 0, "") not in d: return inf
            if k in mixed and kind != "give" and ("take", k, z, "") not in d: return inf
            if kind == "sum" and (z > 0 if way == "u" else z < last): times.append(a.get((way, k, j), inf))
            if kind == "fin":
                if z > 0: times.append(a.get(("u", k, z), inf))
                if z < last: times.append(a.get(("d", k, z), inf))
        elif kind in ("merge", "take"):
            if ("fin" if kind == "merge" else "give", k, z, "y") not in d: return inf
            times.append(a.get(("y", k, z), inf))
        sends = kind in ("own", "sum") or (kind == "fwd" and (z < last if way == "u" else z > 0))
        if sends: times.append(link[z][way] - depth * dur[k])
        return max(times)
    while any(todo):
        best = None
        for z in range(n):
            if not todo[z]: continue
            r = [(ready(z, t), t) for t in todo[z]]
            t0 = max(now[z], min(r)[0])
            if t0 == float("inf"): continue
            if best is None or t0 < best[0]:
                best = (t0, z, min((t for e, t in r if e <= t0), key=lambda t: (rank(z, t), t)))
        t0, z, t = best
        kind, k, j, way = t
        todo[z].remove(t); done[z].add(t); orders[z].append(t)
        spend = {"own": .03, "fwd": .05, "comp": widths[k] / 75.0, "sum": .05, "fin": .05, "merge": .05, "norm": 0.9, "give": .15, "take": .2}[kind]
        now[z] = t0 + spend
        to = None
        if kind == "own" or kind == "fwd": to, tag = z + (1 if way == "u" else -1), ("a", k, j)
        elif kind == "sum": to, tag = z + (1 if way == "u" else -1), (way, k, j)
        elif kind == "give" or (kind == "fin" and k not in mixed): to, tag = z, ("y", k, z)
        if to is not None and 0 <= to <= last:
            start = max(link[z][way], now[z])
            took = dur[k] * (n + 1 if kind == "give" else 1)
            link[z][way] = start + took
            arrive[to][tag] = start + took + lat
    return max(now), orders


def gelu_slope(x):
    cdf = 0.5 * (1.0 + lax.erf(x * 0.7071067811865476))
    return cdf + x * (jnp.exp(-0.5 * x * x) * 0.3989422804014327)


def body(
    n, reps, pieces, mixed,
    partner_ref, count_in, images, cotangent, weights, gain_in, bias_in, ebias_in,
    out_ref,
    gain_ref, bias_ref, ebias_ref, img, cot, par, x, xt, wfull, delta, part, u_in, d_in, u_out, d_out, acc,
    far_out, far_in, mix_out, mix_in,
    count_ref, in_sem, z_recv, y_recv, sent,
):
    z = lax.axis_index("fsdp")
    rep = lax.axis_index("rep")
    partner = {"rep": lax.rem(rep + reps // 2, reps)}
    up, down = {"fsdp": z + 1}, {"fsdp": z - 1}
    last = n - 1
    slots, per_image, width = images.shape
    depth = width // n
    cols = wfull.shape[-1]
    scale = float(width) ** (-0.5)

    _, orders = plan(n, [cols] * pieces, PRI, DEPTH, mixed)
    segments = []
    for order in orders:
        parts = [[]]
        for entry in order:
            if entry[0] in ("norm", "comp"):
                parts.append([])
            else:
                parts[-1].append(entry)
        segments.append(parts)
    early = 1 + max(entry[1] for parts in segments for entry in parts[0])

    def load_cols(lo, hi, sem):
        span = pl.ds(lo * cols, (hi - lo) * cols)
        return pltpu.make_async_copy(weights.at[:, span], par.at[:, span], sem)

    load_w = load_cols(0, early, in_sem.at[0])
    load_rest = load_cols(early, pieces, in_sem.at[6])
    load_x = pltpu.make_async_copy(images, img, in_sem.at[1])
    load_c = pltpu.make_async_copy(cotangent, cot, in_sem.at[2])
    small = [
        pltpu.make_async_copy(gain_in, gain_ref, in_sem.at[3]),
        pltpu.make_async_copy(bias_in, bias_ref, in_sem.at[4]),
        pltpu.make_async_copy(ebias_in, ebias_ref, in_sem.at[5]),
        pltpu.make_async_copy(count_in, count_ref, in_sem.at[7]),
    ]
    load_w.start()

    barrier = pltpu.get_barrier_semaphore()

    @pl.when(z < last)
    def _():
        pl.semaphore_signal(barrier, inc=1, device_id=up, device_id_type=MESH_ID)

    @pl.when(z > 0)
    def _():
        pl.semaphore_signal(barrier, inc=1, device_id=down, device_id_type=MESH_ID)

    pl.semaphore_signal(barrier, inc=1, device_id=partner, device_id_type=MESH_ID)

    load_rest.start()
    load_x.start()
    for load in small:
        load.start()
    load_c.start()

    def cast(k):
        wfull[k, z] = par[:, k * cols:(k + 1) * cols].astype(jnp.bfloat16)

    load_w.wait()
    for k in range(early):
        cast(k)

    peers = 1 + (z > 0).astype(jnp.int32) + (z < last).astype(jnp.int32)
    pl.semaphore_wait(barrier, peers)

    def remote(src, dst, send, recv, to):
        return pltpu.make_async_remote_copy(
            src_ref=src, dst_ref=dst, send_sem=send, recv_sem=recv,
            device_id=to, device_id_type=MESH_ID,
        )

    ag_up, ag_dn, u_send, d_send, y_send = (sent.at[i] for i in range(5))

    def ag_copy(k, s, to, send):
        return remote(wfull.at[k, s], wfull.at[k, s], send, z_recv.at[k, s], to)

    def u_copy(k, j, here):
        return remote(u_out.at[k, j], u_in.at[k, j], u_send, z_recv.at[k, j], up)

    def d_copy(k, j, here):
        sem = z_recv.at[k, n if j == here else j]
        return remote(d_out.at[k, j], d_in.at[k, j], d_send, sem, down)

    def y_copy(k):
        return remote(far_out.at[k], far_in.at[k], y_send, y_recv.at[k], partner)

    def x_copy(k):
        i = mixed.index(k)
        return remote(mix_out.at[i], mix_in.at[i], y_send, y_recv.at[k], partner)

    def norm():
        load_rest.wait()
        for k in range(early, pieces):
            cast(k)
        load_x.wait()
        for load in small:
            load.wait()
        gain = gain_ref[...][None, :]
        shift = bias_ref[...][None, :]
        for i in range(slots):
            rows = img[i].astype(jnp.float32)
            mean = jnp.mean(rows, axis=-1, keepdims=True)
            centered = rows - mean
            var = jnp.mean(centered * centered, axis=-1, keepdims=True)
            v = centered * lax.rsqrt(var + eps_norm) * gain + shift
            x[i] = v.astype(jnp.bfloat16)
            xt[:, i * per_image:(i + 1) * per_image] = v.T.astype(jnp.bfloat16)
        load_c.wait()

    def mix():
        return jnp.where(partner_ref[0] != rep, 0.5, 0.0).astype(jnp.float32)

    def compute(k):
        lo = k * cols
        w = wfull.at[k]
        extra = ebias_ref[lo:lo + cols][None, :]

        count = count_ref[0, z]
        table = w[...].reshape(width, cols)
        for i in range(slots):
            pre = jnp.dot(x[i], table, preferred_element_type=jnp.float32)
            pre = pre * scale + extra
            live = jnp.where(i < count, 1.0, 0.0).astype(jnp.float32)
            cur = cot[i, :, lo:lo + cols].astype(jnp.float32)
            delta[i * per_image:(i + 1) * per_image, :] = (
                cur * gelu_slope(pre) * live
            ).astype(jnp.bfloat16)
        terms = scale * jnp.dot(xt[...], delta[...], preferred_element_type=jnp.float32)
        part[k] = terms.reshape(n, depth, cols)

    def step(me, kind, k, j, way):
        to, send = (up, ag_up) if way == "u" else (down, ag_dn)
        copy, came, out = (u_copy, u_in, u_out) if way == "u" else (d_copy, d_in, d_out)
        final = me == (last if way == "u" else 0)
        first = me == (0 if way == "u" else last)
        if kind == "own":
            ag_copy(k, me, to, send).start()
        elif kind == "fwd":
            ag_copy(k, j, to, send).wait_recv()
            if not final:
                ag_copy(k, j, to, send).start()
        elif kind == "sum":
            total = part[k, j]
            if not first:
                copy(k, j, me).wait_recv()
                total = total + came[k, j].astype(jnp.float32)
            out[k, j] = total.astype(jnp.bfloat16)
            copy(k, j, me + 1 if way == "u" else me - 1).start()
        elif kind == "fin":
            total = part[k, me]
            if me > 0:
                u_copy(k, me, me).wait_recv()
                total = total + u_in[k, me].astype(jnp.float32)
            if me < last:
                d_copy(k, me, me).wait_recv()
                total = total + d_in[k, me].astype(jnp.float32)
            own = par[:, k * cols:(k + 1) * cols]
            if k in mixed:
                own = own + mix() * (mix_in[mixed.index(k), n].astype(jnp.float32) - own)
                out_ref[:, k * cols:(k + 1) * cols] = own - learn_rate * total
                return
            stepped = own - learn_rate * total
            acc[k] = stepped
            far_out[k] = stepped.astype(jnp.bfloat16)
            y_copy(k).start()
        elif kind == "give":
            for i in range(n):
                mix_out[mixed.index(k), i] = part[k, i].astype(jnp.bfloat16)
            mix_out[mixed.index(k), n] = wfull[k, me]
            x_copy(k).start()
        elif kind == "take":
            x_copy(k).wait_recv()
            for i in range(n):
                mine = part[k, i]
                part[k, i] = mine + mix() * (mix_in[mixed.index(k), i].astype(jnp.float32) - mine)
        elif kind == "merge":
            y_copy(k).wait_recv()
            stepped = acc[k]
            out_ref[:, k * cols:(k + 1) * cols] = stepped + mix() * (far_in[k].astype(jnp.float32) - stepped)

    for stage in range(pieces + 2):
        for me in range(n):
            @pl.when(z == me)
            def _():
                for entry in segments[me][stage]:
                    step(me, *entry)
        if stage == 0:
            norm()
        elif stage <= pieces:
            compute(stage - 1)

    def drain(ref, send):
        remote(ref, ref, send, y_recv.at[0], partner).wait_send()

    for me in range(n):
        @pl.when(z == me)
        def _():
            if me < last:
                drain(wfull.at[:, :me + 1], ag_up)
                drain(u_out.at[:, me + 1:], u_send)
            if me > 0:
                drain(wfull.at[:, me:], ag_dn)
                drain(d_out.at[:, :me], d_send)
    drain(far_out.at[len(mixed):], y_send)
    if mixed:
        drain(mix_out, y_send)


def shards(n, reps, images, cotangent, params, counts, partner, ln_gain, ln_bias, expand_bias):
    _, slots, per_image, width = images.shape
    hidden = cotangent.shape[-1]
    depth = params.shape[1]
    cols = CHUNK
    pieces = hidden // cols
    mixed = tuple(k for k in MIXED if k < pieces)
    rows = slots * per_image
    anywhere = pl.BlockSpec(memory_space=pl.ANY)
    dma = pltpu.SemaphoreType.DMA
    bf, f32 = jnp.bfloat16, jnp.float32
    piece = (pieces, n, depth, cols)
    merged = pl.pallas_call(
        functools.partial(body, n, reps, pieces, mixed),
        out_shape=pltpu.VMEM((depth, hidden), f32),
        in_specs=[pl.BlockSpec(memory_space=pltpu.SMEM)] + [anywhere] * 7,
        out_specs=pl.BlockSpec(memory_space=pltpu.VMEM),
        scratch_shapes=[
            pltpu.VMEM((width,), f32),
            pltpu.VMEM((width,), f32),
            pltpu.VMEM((hidden,), f32),
            pltpu.VMEM((slots, per_image, width), bf),
            pltpu.VMEM((slots, per_image, hidden), bf),
            pltpu.VMEM((depth, hidden), f32),
            pltpu.VMEM((slots, per_image, width), bf),
            pltpu.VMEM((width, rows), bf),
            pltpu.VMEM(piece, bf),
            pltpu.VMEM((rows, cols), bf),
            pltpu.VMEM(piece, f32),
            pltpu.VMEM(piece, bf),
            pltpu.VMEM(piece, bf),
            pltpu.VMEM(piece, bf),
            pltpu.VMEM(piece, bf),
            pltpu.VMEM((pieces, depth, cols), f32),
            pltpu.VMEM((pieces, depth, cols), bf),
            pltpu.VMEM((pieces, depth, cols), bf),
            pltpu.VMEM((len(mixed), n + 1, depth, cols), bf),
            pltpu.VMEM((len(mixed), n + 1, depth, cols), bf),
            pltpu.SMEM((1, n), jnp.int32),
            dma((8,)), dma((pieces, n + 1)), dma((pieces,)), dma((5,)),
        ],
        compiler_params=pltpu.CompilerParams(
            collective_id=0, has_side_effects=True, vmem_limit_bytes=32 * 1024 * 1024
        ),
    )(
        partner, *[
            pltpu.with_memory_space_constraint(array, pltpu.HBM)
            for array in (
                counts, images[0], cotangent[0], params[0], ln_gain, ln_bias, expand_bias,
            )
        ],
    )
    return merged[None]


def solution(mesh):
    in_specs = (
        P("rep", "fsdp", None, None),
        P("rep", "fsdp", None, None),
        P("rep", "fsdp", None),
        P("rep", None),
        P("rep"),
        P(),
        P(),
        P(),
    )
    out_specs = P("rep", "fsdp", None)
    return jax.shard_map(
        functools.partial(shards, mesh.shape["fsdp"], mesh.shape["rep"]),
        mesh=mesh, in_specs=in_specs, out_specs=out_specs, check_vma=False,
    )
```

```python
import functools

import jax
import jax.numpy as jnp
from jax import lax
from jax.experimental import pallas as pl
from jax.experimental.pallas import tpu as pltpu
from jax.sharding import PartitionSpec as P

eps_norm = 1e-06
learn_rate = 0.5
CHUNK = 128
DEPTH = 0.00
MIXED = (2, 4, 9,)
PRI = dict(
    give=21.89, take=-114.92, late=96.59, own=24.29, fwd=23.89, fwd_far=-122.00, comp=9.92,
    sum=200.38, sum_far=-215.30, sum_hop=270.01, fin=-88.99, merge=67.96, norm=403.70,
)
MESH_ID = pl.DeviceIdType.MESH


def plan(n, widths, pri, depth, mixed, rate=126.2, lat=2.43, cost=0.055):
    last = n - 1
    pieces = len(widths)
    dur = [w / rate + cost for w in widths]
    arrive = [dict() for _ in range(n)]
    now = [2.0] * n
    link = [dict(u=0.0, d=0.0, y=0.0) for _ in range(n)]
    todo, orders = [], [[] for _ in range(n)]
    for z in range(n):
        mine = []
        for k in range(pieces):
            if z < last: mine.append(("own", k, z, "u"))
            if z > 0: mine.append(("own", k, z, "d"))
            for s in range(n):
                if s != z: mine.append(("fwd", k, s, "u" if s < z else "d"))
            mine.append(("comp", k, 0, ""))
            for j in range(z + 1, n): mine.append(("sum", k, j, "u"))
            for j in range(z): mine.append(("sum", k, j, "d"))
            mine.append(("fin", k, z, "y"))
            if k in mixed:
                mine.append(("give", k, z, "y"))
                mine.append(("take", k, z, ""))
            else:
                mine.append(("merge", k, z, ""))
        mine.append(("norm", 0, 0, ""))
        todo.append(mine)
    done = [set() for _ in range(n)]
    def rank(z, t):
        kind, k, j, way = t
        far = abs(j - z)
        if kind == "own": return k + pri["own"]
        if kind == "fwd": return k + pri["fwd"] + (far - 1) * pri["fwd_far"]
        if kind == "sum": return k + (pri["late"] if k in mixed else 0.0) + pri["sum"] + far * pri["sum_far"] + (z if way == "u" else last - z) * pri["sum_hop"]
        return k + pri.get(kind, 0.0)
    def ready(z, t):
        kind, k, j, way = t
        a, d = arrive[z], done[z]
        times = [0.0]
        inf = float("inf")
        if kind == "fwd":
            times.append(a.get(("a", k, j), inf))
        elif kind == "comp":
            if ("norm", 0, 0, "") not in d: return inf
            if k and ("comp", k - 1, 0, "") not in d: return inf
            for s in range(n):
                if s != z and ("fwd", k, s, "u" if s < z else "d") not in d: return inf
        elif kind in ("sum", "fin", "give"):
            if ("comp", k, 0, "") not in d: return inf
            if k in mixed and kind != "give" and ("take", k, z, "") not in d: return inf
            if kind == "sum" and (z > 0 if way == "u" else z < last): times.append(a.get((way, k, j), inf))
            if kind == "fin":
                if z > 0: times.append(a.get(("u", k, z), inf))
                if z < last: times.append(a.get(("d", k, z), inf))
        elif kind in ("merge", "take"):
            if ("fin" if kind == "merge" else "give", k, z, "y") not in d: return inf
            times.append(a.get(("y", k, z), inf))
        sends = kind in ("own", "sum") or (kind == "fwd" and (z < last if way == "u" else z > 0))
        if sends: times.append(link[z][way] - depth * dur[k])
        return max(times)
    while any(todo):
        best = None
        for z in range(n):
            if not todo[z]: continue
            r = [(ready(z, t), t) for t in todo[z]]
            t0 = max(now[z], min(r)[0])
            if t0 == float("inf"): continue
            if best is None or t0 < best[0]:
                best = (t0, z, min((t for e, t in r if e <= t0), key=lambda t: (rank(z, t), t)))
        t0, z, t = best
        kind, k, j, way = t
        todo[z].remove(t); done[z].add(t); orders[z].append(t)
        spend = {"own": .03, "fwd": .05, "comp": widths[k] / 142.0, "sum": .05, "fin": .05, "merge": .05, "norm": 0.9, "give": .07, "take": .1}[kind]
        now[z] = t0 + spend
        to = None
        if kind == "own" or kind == "fwd": to, tag = z + (1 if way == "u" else -1), ("a", k, j)
        elif kind == "sum": to, tag = z + (1 if way == "u" else -1), (way, k, j)
        elif kind == "give" or (kind == "fin" and k not in mixed): to, tag = z, ("y", k, z)
        if to is not None and 0 <= to <= last:
            start = max(link[z][way], now[z])
            took = dur[k] * (n + 1 if kind == "give" else 1)
            link[z][way] = start + took
            arrive[to][tag] = start + took + lat
    return max(now), orders


def gelu_slope(x):
    cdf = 0.5 * (1.0 + lax.erf(x * 0.7071067811865476))
    return cdf + x * (jnp.exp(-0.5 * x * x) * 0.3989422804014327)


def body(
    n, reps, pieces, mixed,
    partner_ref, count_in, images, cotangent, weights, gain_in, bias_in, ebias_in,
    out_ref,
    gain_ref, bias_ref, ebias_ref, img, cot, par, x, xt, wfull, delta, part, u_in, d_in, u_out, d_out, acc,
    far_out, far_in, mix_out, mix_in,
    count_ref, in_sem, z_recv, y_recv, sent,
):
    z = lax.axis_index("fsdp")
    rep = lax.axis_index("rep")
    partner = {"rep": lax.rem(rep + reps // 2, reps)}
    up, down = {"fsdp": z + 1}, {"fsdp": z - 1}
    last = n - 1
    slots, per_image, width = images.shape
    depth = width // n
    cols = wfull.shape[-1]
    scale = float(width) ** (-0.5)

    _, orders = plan(n, [cols] * pieces, PRI, DEPTH, mixed)
    segments = []
    for order in orders:
        parts = [[]]
        for entry in order:
            if entry[0] in ("norm", "comp"):
                parts.append([])
            else:
                parts[-1].append(entry)
        segments.append(parts)
    early = 1 + max(entry[1] for parts in segments for entry in parts[0])

    def load_cols(lo, hi, sem):
        span = pl.ds(lo * cols, (hi - lo) * cols)
        return pltpu.make_async_copy(weights.at[:, span], par.at[:, span], sem)

    load_w = load_cols(0, early, in_sem.at[0])
    load_rest = load_cols(early, pieces, in_sem.at[6])
    load_x = pltpu.make_async_copy(images, img, in_sem.at[1])
    load_c = pltpu.make_async_copy(cotangent, cot, in_sem.at[2])
    small = [
        pltpu.make_async_copy(gain_in, gain_ref, in_sem.at[3]),
        pltpu.make_async_copy(bias_in, bias_ref, in_sem.at[4]),
        pltpu.make_async_copy(ebias_in, ebias_ref, in_sem.at[5]),
        pltpu.make_async_copy(count_in, count_ref, in_sem.at[7]),
    ]
    load_w.start()

    barrier = pltpu.get_barrier_semaphore()

    @pl.when(z < last)
    def _():
        pl.semaphore_signal(barrier, inc=1, device_id=up, device_id_type=MESH_ID)

    @pl.when(z > 0)
    def _():
        pl.semaphore_signal(barrier, inc=1, device_id=down, device_id_type=MESH_ID)

    pl.semaphore_signal(barrier, inc=1, device_id=partner, device_id_type=MESH_ID)

    load_rest.start()
    load_x.start()
    for load in small:
        load.start()
    load_c.start()

    def cast(k):
        wfull[k, z] = par[:, k * cols:(k + 1) * cols].astype(jnp.bfloat16)

    load_w.wait()
    for k in range(early):
        cast(k)

    peers = 1 + (z > 0).astype(jnp.int32) + (z < last).astype(jnp.int32)
    pl.semaphore_wait(barrier, peers)

    def remote(src, dst, send, recv, to):
        return pltpu.make_async_remote_copy(
            src_ref=src, dst_ref=dst, send_sem=send, recv_sem=recv,
            device_id=to, device_id_type=MESH_ID,
        )

    ag_up, ag_dn, u_send, d_send, y_send = (sent.at[i] for i in range(5))

    def ag_copy(k, s, to, send):
        return remote(wfull.at[k, s], wfull.at[k, s], send, z_recv.at[k, s], to)

    def u_copy(k, j, here):
        return remote(u_out.at[k, j], u_in.at[k, j], u_send, z_recv.at[k, j], up)

    def d_copy(k, j, here):
        sem = z_recv.at[k, n if j == here else j]
        return remote(d_out.at[k, j], d_in.at[k, j], d_send, sem, down)

    def y_copy(k):
        return remote(far_out.at[k], far_in.at[k], y_send, y_recv.at[k], partner)

    def x_copy(k):
        i = mixed.index(k)
        return remote(mix_out.at[i], mix_in.at[i], y_send, y_recv.at[k], partner)

    def norm():
        load_rest.wait()
        for k in range(early, pieces):
            cast(k)
        load_x.wait()
        for load in small:
            load.wait()
        gain = gain_ref[...][None, :]
        shift = bias_ref[...][None, :]
        for i in range(slots):
            rows = img[i].astype(jnp.float32)
            mean = jnp.mean(rows, axis=-1, keepdims=True)
            centered = rows - mean
            var = jnp.mean(centered * centered, axis=-1, keepdims=True)
            v = centered * lax.rsqrt(var + eps_norm) * gain + shift
            x[i] = v.astype(jnp.bfloat16)
            xt[:, i * per_image:(i + 1) * per_image] = v.T.astype(jnp.bfloat16)
        load_c.wait()

    def mix():
        return jnp.where(partner_ref[0] != rep, 0.5, 0.0).astype(jnp.float32)

    def compute(k):
        lo = k * cols
        w = wfull.at[k]
        extra = ebias_ref[lo:lo + cols][None, :]

        count = count_ref[0, z]
        table = w[...].reshape(width, cols)
        for i in range(slots):
            pre = jnp.dot(x[i], table, preferred_element_type=jnp.float32)
            pre = pre * scale + extra
            live = jnp.where(i < count, 1.0, 0.0).astype(jnp.float32)
            cur = cot[i, :, lo:lo + cols].astype(jnp.float32)
            delta[i * per_image:(i + 1) * per_image, :] = (
                cur * gelu_slope(pre) * live
            ).astype(jnp.bfloat16)
        terms = scale * jnp.dot(xt[...], delta[...], preferred_element_type=jnp.float32)
        part[k] = terms.reshape(n, depth, cols)

    def step(me, kind, k, j, way):
        to, send = (up, ag_up) if way == "u" else (down, ag_dn)
        copy, came, out = (u_copy, u_in, u_out) if way == "u" else (d_copy, d_in, d_out)
        final = me == (last if way == "u" else 0)
        first = me == (0 if way == "u" else last)
        if kind == "own":
            ag_copy(k, me, to, send).start()
        elif kind == "fwd":
            ag_copy(k, j, to, send).wait_recv()
            if not final:
                ag_copy(k, j, to, send).start()
        elif kind == "sum":
            total = part[k, j]
            if not first:
                copy(k, j, me).wait_recv()
                total = total + came[k, j].astype(jnp.float32)
            out[k, j] = total.astype(jnp.bfloat16)
            copy(k, j, me + 1 if way == "u" else me - 1).start()
        elif kind == "fin":
            total = part[k, me]
            if me > 0:
                u_copy(k, me, me).wait_recv()
                total = total + u_in[k, me].astype(jnp.float32)
            if me < last:
                d_copy(k, me, me).wait_recv()
                total = total + d_in[k, me].astype(jnp.float32)
            own = par[:, k * cols:(k + 1) * cols]
            if k in mixed:
                own = own + mix() * (mix_in[mixed.index(k), n].astype(jnp.float32) - own)
                out_ref[:, k * cols:(k + 1) * cols] = own - learn_rate * total
                return
            stepped = own - learn_rate * total
            acc[k] = stepped
            far_out[k] = stepped.astype(jnp.bfloat16)
            y_copy(k).start()
        elif kind == "give":
            for i in range(n):
                mix_out[mixed.index(k), i] = part[k, i].astype(jnp.bfloat16)
            mix_out[mixed.index(k), n] = wfull[k, me]
            x_copy(k).start()
        elif kind == "take":
            x_copy(k).wait_recv()
            for i in range(n):
                mine = part[k, i]
                part[k, i] = mine + mix() * (mix_in[mixed.index(k), i].astype(jnp.float32) - mine)
        elif kind == "merge":
            y_copy(k).wait_recv()
            stepped = acc[k]
            out_ref[:, k * cols:(k + 1) * cols] = stepped + mix() * (far_in[k].astype(jnp.float32) - stepped)

    for stage in range(pieces + 2):
        for me in range(n):
            @pl.when(z == me)
            def _():
                for entry in segments[me][stage]:
                    step(me, *entry)
        if stage == 0:
            norm()
        elif stage <= pieces:
            compute(stage - 1)

    def drain(ref, send):
        remote(ref, ref, send, y_recv.at[0], partner).wait_send()

    for me in range(n):
        @pl.when(z == me)
        def _():
            if me < last:
                drain(wfull.at[:, :me + 1], ag_up)
                drain(u_out.at[:, me + 1:], u_send)
            if me > 0:
                drain(wfull.at[:, me:], ag_dn)
                drain(d_out.at[:, :me], d_send)
    drain(far_out.at[len(mixed):], y_send)
    if mixed:
        drain(mix_out, y_send)


def shards(n, reps, images, cotangent, params, counts, partner, ln_gain, ln_bias, expand_bias):
    _, slots, per_image, width = images.shape
    hidden = cotangent.shape[-1]
    depth = params.shape[1]
    cols = CHUNK
    pieces = hidden // cols
    mixed = tuple(k for k in MIXED if k < pieces)
    rows = slots * per_image
    anywhere = pl.BlockSpec(memory_space=pl.ANY)
    dma = pltpu.SemaphoreType.DMA
    bf, f32 = jnp.bfloat16, jnp.float32
    piece = (pieces, n, depth, cols)
    merged = pl.pallas_call(
        functools.partial(body, n, reps, pieces, mixed),
        out_shape=pltpu.VMEM((depth, hidden), f32),
        in_specs=[pl.BlockSpec(memory_space=pltpu.SMEM)] + [anywhere] * 7,
        out_specs=pl.BlockSpec(memory_space=pltpu.VMEM),
        scratch_shapes=[
            pltpu.VMEM((width,), f32),
            pltpu.VMEM((width,), f32),
            pltpu.VMEM((hidden,), f32),
            pltpu.VMEM((slots, per_image, width), bf),
            pltpu.VMEM((slots, per_image, hidden), bf),
            pltpu.VMEM((depth, hidden), f32),
            pltpu.VMEM((slots, per_image, width), bf),
            pltpu.VMEM((width, rows), bf),
            pltpu.VMEM(piece, bf),
            pltpu.VMEM((rows, cols), bf),
            pltpu.VMEM(piece, f32),
            pltpu.VMEM(piece, bf),
            pltpu.VMEM(piece, bf),
            pltpu.VMEM(piece, bf),
            pltpu.VMEM(piece, bf),
            pltpu.VMEM((pieces, depth, cols), f32),
            pltpu.VMEM((pieces, depth, cols), bf),
            pltpu.VMEM((pieces, depth, cols), bf),
            pltpu.VMEM((len(mixed), n + 1, depth, cols), bf),
            pltpu.VMEM((len(mixed), n + 1, depth, cols), bf),
            pltpu.SMEM((1, n), jnp.int32),
            dma((8,)), dma((pieces, n + 1)), dma((pieces,)), dma((5,)),
        ],
        compiler_params=pltpu.CompilerParams(
            collective_id=0, has_side_effects=True, vmem_limit_bytes=32 * 1024 * 1024
        ),
    )(
        partner, *[
            pltpu.with_memory_space_constraint(array, pltpu.HBM)
            for array in (
                counts, images[0], cotangent[0], params[0], ln_gain, ln_bias, expand_bias,
            )
        ],
    )
    return merged[None]


def solution(mesh):
    in_specs = (
        P("rep", "fsdp", None, None),
        P("rep", "fsdp", None, None),
        P("rep", "fsdp", None),
        P("rep", None),
        P("rep"),
        P(),
        P(),
        P(),
    )
    out_specs = P("rep", "fsdp", None)
    return jax.shard_map(
        functools.partial(shards, mesh.shape["fsdp"], mesh.shape["rep"]),
        mesh=mesh, in_specs=in_specs, out_specs=out_specs, check_vma=False,
    )
```
